32 devices in a mesh: groups: 2 (over y), dp: 4 (over z), mp: 4 (over x, core).
Axes of the slice: x: 2, y: 2, z: 4, core: 2. Of those that a mesh axis runs over, the one named last changes fastest.
Arguments:
- qkv_home: bfloat16 [8, 764, 3, 3072], P(('groups', 'dp'), None, None, 'mp'), parts along dimension 0, may hold values from -6 to 6
- resid_home: bfloat16 [8, 764, 6144], P(('groups', 'dp'), None, 'mp'), parts along dimension 0, may hold values from -6 to 6
- out_weight: bfloat16 [3072, 6144], P('dp', 'mp'), may hold values from -0.109375 to 0.109375
- label_weight: bfloat16 [6144, 12288], P('mp', 'dp'), may hold values from -0.21875 to 0.21875
- label_bias: float32 [12288], P('dp'), may hold values from -5 to 5
- query_gain: float32 [128], replicated, may hold values from 0.25 to 1.75
- key_gain: float32 [128], replicated, may hold values from 0.25 to 1.75
- patch_counts: int32 [8, 4], P('groups'), parts along dimension 0, may hold values from 1 to 191, as said below
- move_plan: int32 [8, 4], P('groups'), parts along dimension 0, may hold values from 0 to 3, as said below
- segment_ids: int32 [8, 764], P(('groups', 'dp')), parts along dimension 0, may hold values from 0 to 4, as said below
Outputs:
- mixed: bfloat16 [8, 384, 6144], P(('groups', 'dp'), None, 'mp'), parts along dimension 0
- labels: float32 [8, 4, 12288], P(('groups', 'dp'), 'mp'), parts along dimension 0
The draws below stay inside these ranges and needn't reach their ends.
There are 2 independent parts, one for each index of `groups`. The reference program is written for one: setup_inputs(seed, part) draws one part's arguments, and reference() takes and returns one part's arrays. A program takes and returns all parts, laid end to end along the dimension named above; an argument that names none is the same for every part. Nothing has to cross between parts.
Inputs may be any that keep to these rules, and one draw needn't show every extreme that they name: `patch_counts`: home row r holds its 4 images packed in the order j; every destination row receives exactly one image from every home row, 384 patches in all; every draw holds an image of 191 patches. Every row of move_plan is a permutation, and every destination row appears once in every column, so each destination receives one image from each home row. `segment_ids`: image j of home row r has id j on its patch_counts[r, j] slots, which follow those of image j - 1; slots after the last image have id 4.
All inputs are finite; a program needn't handle non-finite values.
Results may differ from the reference program's by a relative error of at most 0.0065.
Values may be sent and summed in bfloat16 or wider, within the bound.
A program may use at most 64 MiB of HBM per device.

```python
import math
import jax
import jax.numpy as jnp
from jax import lax

D = 6144
HD = 128
HEADS = 24
CLASSES = 12288
TOK = 384
ROWS = 4
MEAN = 96
HOME = 764


def draw_layout(key):
    base_key = jax.random.fold_in(key, 7)
    sub_keys = jax.random.split(base_key, 6)
    row_ids = jnp.arange(ROWS, dtype=jnp.int32)
    col_shift = jax.random.permutation(sub_keys[0], ROWS).astype(jnp.int32)
    row_shift = jax.random.permutation(sub_keys[1], ROWS).astype(jnp.int32)
    move_plan = (col_shift[None, :] + row_shift[:, None]) % ROWS
    pairing = jax.random.permutation(sub_keys[2], ROWS).astype(jnp.int32)
    centers = jax.random.randint(sub_keys[3], (ROWS // 2, 1), 1, 2 * MEAN)
    jitter = jax.random.randint(sub_keys[4], (ROWS // 2, ROWS), -(MEAN // 2), MEAN // 2 + 1)
    heavy = jnp.clip(centers + jitter, 1, 2 * MEAN - 1)
    full_dest = jax.random.randint(sub_keys[5], (ROWS // 2, 1), 0, ROWS)
    heavy = jnp.where(row_ids[None, :] == full_dest, 2 * MEAN - 1, heavy).astype(jnp.int32)
    loads = jnp.zeros((ROWS, ROWS), jnp.int32)
    loads = loads.at[pairing[0::2]].set(heavy)
    loads = loads.at[pairing[1::2]].set(2 * MEAN - heavy)
    counts = jnp.take_along_axis(loads, move_plan, axis=1)
    image_ends = jnp.cumsum(counts, axis=1)
    slot_ids = jnp.arange(HOME, dtype=jnp.int32)
    segments = jnp.sum((slot_ids[None, :, None] >= image_ends[:, None, :]).astype(jnp.int32), axis=2)
    return (counts.astype(jnp.int32), move_plan.astype(jnp.int32), segments.astype(jnp.int32))


def draw_patch_counts(key, part):
    return draw_layout(key)[0]


def draw_move_plan(key, part):
    return draw_layout(key)[1]


def draw_segment_ids(key, part):
    return draw_layout(key)[2]


def steps_of(own_key, dims, cuts, low, largest):
    factor_of, own = 1.0, jax.random.fold_in(own_key, 6)
    for axis_at, parts in cuts:
        heights = jnp.exp(jax.random.uniform(jax.random.fold_in(own, axis_at), (parts,), jnp.float32, low / len(cuts), largest / len(cuts)))
        factor_of = factor_of * jnp.repeat(heights, dims[axis_at] // parts).reshape([-1 if axis == axis_at else 1 for axis in range(len(dims))])
    return factor_of


def centred(rng, shape, width, bound, cuts=(), held_as=jnp.bfloat16):
    factor_of = steps_of(rng, shape, cuts, -0.22, 0.18) if cuts else 1.0
    result = jax.random.normal(rng, shape, jnp.float32) * width * factor_of
    return jnp.minimum(jnp.maximum(result, -bound), bound).astype(held_as)


def setup_inputs(seed: int = 0, part: int = 0) -> dict:
    key_of = jax.random.split(jax.random.key(seed), 11)
    part_keys = jax.random.split(jax.random.fold_in(key_of[10], part), 11)
    return {
        "qkv_home": centred(part_keys[0], (ROWS, HOME, 3, HEADS * HD), 1.0, 6.0, ((0, 4), (3, 4))),
        "resid_home": centred(part_keys[1], (ROWS, HOME, D), 1.0, 6.0, ((0, 4), (2, 4))),
        "out_weight": centred(key_of[2], (HEADS * HD, D), (HEADS * HD) ** -0.5, 0.109375, ((0, 4), (1, 4))),
        "label_weight": centred(key_of[3], (D, CLASSES), (D // 8) ** -0.5, 0.21875, ((0, 4), (1, 4))),
        "label_bias": centred(key_of[4], (CLASSES,), 1.0, 5.0, ((0, 4),), jnp.float32),
        "query_gain": jnp.clip(1.0 + 0.15 * jax.random.normal(key_of[5], (HD,), jnp.float32), 0.25, 1.75),
        "key_gain": jnp.clip(1.0 + 0.15 * jax.random.normal(key_of[6], (HD,), jnp.float32), 0.25, 1.75),
        "patch_counts": draw_patch_counts(jax.random.fold_in(jax.random.fold_in(key_of[10], part), 71), part),
        "move_plan": draw_move_plan(jax.random.fold_in(jax.random.fold_in(key_of[10], part), 71), part),
        "segment_ids": draw_segment_ids(jax.random.fold_in(jax.random.fold_in(key_of[10], part), 71), part),
    }


EPSILON = 1e-06

def head_norm(values, norm_gain):
    center = values - lax.optimization_barrier(jnp.mean(values, axis=-1, keepdims=True))
    spread = lax.optimization_barrier(jnp.mean(center * center, axis=-1, keepdims=True))
    return center * lax.rsqrt(spread + EPSILON) * norm_gain

def rounded(values):
    return lax.optimization_barrier(values.astype(jnp.bfloat16)).astype(jnp.float32)

def attend(qkv_rows, seg_rows, query_gain, key_gain):
    length = qkv_rows.shape[0]
    head_count = qkv_rows.shape[2] // HD
    split_parts = qkv_rows.astype(jnp.float32).reshape(length, 3, head_count, HD)
    queries = rounded(head_norm(split_parts[:, 0], query_gain))
    key_rows = rounded(head_norm(split_parts[:, 1], key_gain))
    scores = jnp.einsum('qhd,khd->hqk', queries, key_rows) / math.sqrt(HD)
    same_image = (seg_rows[:, None] == seg_rows[None, :]).astype(jnp.float32)
    raised = jnp.exp(scores) * same_image[None]
    weights = rounded(raised / lax.optimization_barrier(jnp.sum(raised, axis=-1, keepdims=True)))
    head_out = jnp.einsum('hqk,khd->qhd', weights, split_parts[:, 2])
    return head_out.reshape(length, head_count * HD).astype(jnp.bfloat16)

def reference(qkv_home, resid_home, out_weight, label_weight, label_bias, query_gain, key_gain, patch_counts, move_plan, segment_ids):
    row_count = patch_counts.shape[0]
    home_slots = qkv_home.shape[1]
    image_ids = jnp.arange(row_count, dtype=jnp.int32)

    def one_row(entry):
        qkv_rows, resid_rows, seg_rows, count_row = entry
        heads_done = attend(qkv_rows, seg_rows, query_gain, key_gain)
        projected = jnp.dot(heads_done, out_weight, preferred_element_type=jnp.float32)
        row_mixed = (resid_rows.astype(jnp.float32) + projected).astype(jnp.bfloat16)
        member = (image_ids[:, None] == seg_rows[None, :]).astype(jnp.bfloat16)
        image_sums = jnp.dot(member, row_mixed, preferred_element_type=jnp.float32)
        row_pooled = (image_sums / count_row[:, None].astype(jnp.float32)).astype(jnp.bfloat16)
        return (row_mixed, row_pooled)
    home_mixed, pooled = lax.map(one_row, (qkv_home, resid_home, segment_ids, patch_counts))
    logits = jnp.dot(pooled.reshape(row_count * row_count, -1), label_weight, preferred_element_type=jnp.float32)
    logits = logits + label_bias.astype(jnp.float32)[None, :]
    labels = jax.nn.sigmoid(logits).reshape(row_count, row_count, -1)
    image_ends = jnp.cumsum(patch_counts, axis=1)
    starts = image_ends - patch_counts
    matches = (move_plan[:, :, None] == image_ids[None, None, :]).astype(jnp.int32)
    image_sizes = lax.optimization_barrier(jnp.sum(patch_counts[:, :, None] * matches, axis=1))
    firsts = lax.optimization_barrier(jnp.sum(starts[:, :, None] * matches, axis=1))
    column_ends = jnp.cumsum(image_sizes, axis=0)
    column_starts = column_ends - image_sizes
    slot_ids = jnp.arange(TOK, dtype=jnp.int32)
    source = lax.optimization_barrier(jnp.sum((slot_ids[None, :, None] >= column_ends.T[:, None, :]).astype(jnp.int32), axis=2))
    chosen = (source[:, :, None] == image_ids[None, None, :]).astype(jnp.int32)
    shift_by = lax.optimization_barrier(jnp.sum(chosen * (firsts.T[:, None, :] - column_starts.T[:, None, :]), axis=2))
    flat_index = (source * home_slots + shift_by + slot_ids[None, :]).astype(jnp.int32)
    mixed = jnp.take(home_mixed.reshape(row_count * home_slots, -1), flat_index.reshape(-1), axis=0)
    mixed = mixed.reshape(row_count, TOK, -1)
    return (mixed, labels)
```

```python
import functools
import math

import jax
import jax.numpy as jnp
from jax import lax
from jax.experimental import pallas as pl
from jax.experimental.pallas import tpu as pltpu
from jax.sharding import PartitionSpec as P

TOK = 384


EPSILON = 1e-06


def head_norm(values, norm_gain):
    center = values - jnp.mean(values, axis=-1, keepdims=True)
    spread = jnp.mean(center * center, axis=-1, keepdims=True)
    return center * lax.rsqrt(spread + EPSILON) * norm_gain


def attend(qkv_rows, seg_rows, query_gain, key_gain):
    length = qkv_rows.shape[0]
    head_width = query_gain.shape[0]
    head_count = qkv_rows.shape[2] // head_width
    split_parts = qkv_rows.reshape(length, 3, head_count, head_width)
    queries = head_norm(split_parts[:, 0].astype(jnp.float32), query_gain).astype(jnp.bfloat16)
    key_rows = head_norm(split_parts[:, 1].astype(jnp.float32), key_gain).astype(jnp.bfloat16)
    scores = jnp.einsum(
        "qhd,khd->hqk", queries, key_rows, preferred_element_type=jnp.float32
    ) / math.sqrt(head_width)
    same_image = seg_rows[:, None] == seg_rows[None, :]
    raised = jnp.where(same_image[None], jnp.exp(scores), 0.0)
    weights = (raised / jnp.sum(raised, axis=-1, keepdims=True)).astype(jnp.bfloat16)
    head_out = jnp.einsum(
        "hqk,khd->qhd", weights, split_parts[:, 2], preferred_element_type=jnp.float32
    )
    return head_out.reshape(length, head_count * head_width).astype(jnp.bfloat16)


def project(heads_local, resid_rows, out_weight):
    gathered = lax.all_gather(heads_local, "mp", axis=1, tiled=True)
    running = resid_rows.astype(jnp.float32) + jnp.dot(
        gathered,
        lax.all_gather(out_weight, "dp", axis=0, tiled=True),
        preferred_element_type=jnp.float32,
    )
    return running.astype(jnp.bfloat16)


def pool(row_mixed, seg_rows, count_row):
    images = count_row.shape[0]
    member_ids = lax.broadcasted_iota(jnp.int32, (images, seg_rows.shape[0]), 0)
    member = (member_ids == seg_rows[None, :]).astype(jnp.bfloat16)
    image_sums = jnp.dot(member, row_mixed, preferred_element_type=jnp.float32)
    return (image_sums / count_row[:, None].astype(jnp.float32)).astype(jnp.bfloat16)


def label_terms(pooled, label_weight):
    return jnp.einsum(
        "abd,dc->abc",
        lax.all_gather(pooled[None], "dp", axis=0, tiled=True),
        label_weight,
        preferred_element_type=jnp.float32,
    )


def pick(values, row_index, is_valid):
    taken = jnp.take(values, row_index, axis=0)
    taken = taken.reshape(is_valid.shape + values.shape[1:])
    keep_mask = is_valid.reshape(is_valid.shape + (1,) * (values.ndim - 1))
    return jnp.where(keep_mask, taken, jnp.zeros_like(taken))


MESH = pl.DeviceIdType.MESH
LANES = 128
TILE = 256


def remote(src, dst, send_sem, recv_sem, where):
    return pltpu.make_async_remote_copy(
        src_ref=src,
        dst_ref=dst,
        send_sem=send_sem,
        recv_sem=recv_sem,
        device_id=where,
        device_id_type=MESH,
    )


def normed(values, gain):
    values = values.astype(jnp.float32)
    center = values - jnp.mean(values, axis=-1, keepdims=True)
    spread = jnp.mean(center * center, axis=-1, keepdims=True)
    return (center * lax.rsqrt(spread + EPSILON) * gain).astype(jnp.bfloat16)


def block_kernel(
    sizes,
    counts,
    plan,
    q_ref,
    k_ref,
    v_ref,
    bias_ref,
    qg_ref,
    kg_ref,
    resid_hbm,
    w_hbm,
    lw_hbm,
    out_ref,
    lab_ref,
    nq,
    nk,
    hall,
    wall,
    acc,
    mixed,
    sbuf,
    rbuf,
    lwv,
    resv,
    pools,
    lgs,
    lrecv,
    pbuf,
    precv,
    load_sem,
    hs,
    hr,
    wzs,
    wzr,
    wys,
    wyr,
    ps,
    pr,
    ms,
    mr,
    ls,
    lr,
    bs,
    br,
):
    rows, slots, pair = sizes
    me = lax.axis_index("dp")
    mp = lax.axis_index("mp")
    group = lax.axis_index("groups")
    other = 1 - group
    core = lax.rem(mp, 2)
    near = mp + 1 - 2 * core
    side = lax.rem(mp + 2, 4)
    far = lax.rem(near + 2, 4)
    length, width = q_ref.shape
    depth, cols = w_hbm.shape
    half = cols // 2
    pieces = width // TILE
    images = rows

    loads = [
        pltpu.make_async_copy(w_hbm, wall.at[me], load_sem.at[0]),
        pltpu.make_async_copy(resid_hbm, resv, load_sem.at[1]),
        pltpu.make_async_copy(lw_hbm, lwv, load_sem.at[2]),
    ]
    for load in loads:
        load.start()

    barrier = pltpu.get_barrier_semaphore()
    for k in range(1, 4):
        pl.semaphore_signal(
            barrier, inc=1, device_id={"mp": lax.rem(mp + k, 4)}, device_id_type=MESH
        )
    for k in range(1, rows):
        pl.semaphore_signal(
            barrier, inc=1, device_id={"dp": lax.rem(me + k, rows)}, device_id_type=MESH
        )
    pl.semaphore_signal(barrier, inc=1, device_id={"groups": other}, device_id_type=MESH)
    pl.semaphore_wait(barrier, 3 + rows - 1 + 1)

    def wpart(block, which, c):
        return wall.at[block, pl.ds(c * TILE, TILE), pl.ds(pl.multiple_of(which * half, half), half)]

    def own_part(c):
        return w_hbm.at[pl.ds(c * TILE, TILE), pl.ds(pl.multiple_of(group * half, half), half)]

    def zcopy(direction, step, c):
        block = me - step if direction == 0 else me + step
        peer = me + 1 if direction == 0 else me - 1
        return remote(
            own_part(c) if step == 0 else wpart(block, group, c),
            wpart(block, group, c),
            wzs.at[direction, step, c],
            wzr.at[block, c],
            {"dp": peer},
        )

    def can_send(direction, step):
        if direction == 0:
            return jnp.logical_and(me - step >= 0, me < rows - 1)
        return jnp.logical_and(me + step < rows, me > 0)

    def arrives(direction, step):
        return me - step >= 0 if direction == 0 else me + step < rows

    def ycopy(direction, step, c):
        block = me - step if direction == 0 else me + step
        part = wpart(block, group, c)
        return remote(part, part, wys.at[direction, step, c], wyr.at[block, c], {"groups": other})

    chunks = depth // TILE
    for c in range(chunks):
        for direction in range(2):

            @pl.when(can_send(direction, 0))
            def _(direction=direction, c=c):
                zcopy(direction, 0, c).start()

    def forward(step, c):
        for direction in range(2):

            @pl.when(arrives(direction, step))
            def _(direction=direction):
                block = me - step if direction == 0 else me + step
                got = wpart(block, group, c)
                remote(got, got, wzs.at[0, 0, 0], wzr.at[block, c], {"groups": other}).wait_recv()
                ycopy(direction, step, c).start()
                if step < rows - 1:

                    @pl.when(can_send(direction, step))
                    def _():
                        zcopy(direction, step, c).start()

    own_counts = [counts[me, j] for j in range(images)]
    own_plan = [plan[me, j] for j in range(images)]
    ends, starts, running = [], [], 0
    for j in range(images):
        starts.append(running)
        running = running + own_counts[j]
        ends.append(running)

    def segment(index):
        total = jnp.zeros(index.shape, jnp.int32)
        for j in range(images):
            total = total + (index >= ends[j]).astype(jnp.int32)
        return total

    key_seg = segment(lax.broadcasted_iota(jnp.int32, (1, length), 1))
    heads = width // LANES
    q_gain = qg_ref[...]
    k_gain = kg_ref[...]

    def norm_head(h, carry):
        at = pl.ds(pl.multiple_of(h * LANES, LANES), LANES)
        nq[:, at] = normed(q_ref[:, at], q_gain)
        nk[:, at] = normed(k_ref[:, at], k_gain)
        return carry

    lax.fori_loop(0, heads, norm_head, 0)
    scale = math.log2(math.e) / math.sqrt(LANES)
    per_head = length // TILE

    def hcopy(kind, p):
        at = pl.ds(p * TILE, TILE)
        block = side if kind == 2 else mp
        part = hall.at[block, :, at]
        peer = side if kind == 1 else near
        return remote(part, part, hs.at[kind, p], hr.at[kind, p], {"mp": peer})

    def hwait(kind, p):
        block = (near, side, far)[kind]
        part = hall.at[block, :, pl.ds(p * TILE, TILE)]
        remote(part, part, hs.at[kind, p], hr.at[kind, p], {"mp": near}).wait_recv()

    for p in range(pieces):

        def attend_part(i, carry, p=p):
            h = p * (TILE // LANES) + i // per_head
            first = pl.multiple_of(lax.rem(i, per_head) * TILE, TILE)
            at = pl.ds(pl.multiple_of(h * LANES, LANES), LANES)
            scores = lax.dot_general(
                nq[pl.ds(first, TILE), at],
                nk[:, at],
                (((1,), (1,)), ((), ())),
                preferred_element_type=jnp.float32,
            )
            query_seg = segment(lax.broadcasted_iota(jnp.int32, (TILE, 1), 0) + first)
            raised = jnp.where(query_seg == key_seg, jnp.exp2(scores * scale), 0.0)
            total = jnp.sum(raised, axis=-1, keepdims=True)
            weights = (raised * (1.0 / total)).astype(jnp.bfloat16)
            result = jnp.dot(weights, v_ref[:, at], preferred_element_type=jnp.float32)
            hall[mp, pl.ds(first, TILE), at] = result.astype(jnp.bfloat16)
            return carry

        lax.fori_loop(0, (TILE // LANES) * per_head, attend_part, 0)
        hcopy(1, p).start()
        hcopy(0, p).start()
        if p < chunks:
            forward(1, p)
    for c in range(pieces, chunks):
        forward(1, c)
    for p in range(pieces):
        hwait(1, p)
        hcopy(2, p).start()
    for p in range(pieces):
        hwait(0, p)
        hwait(2, p)

    def add_block(block, fresh):
        def tile(t, carry):
            at = pl.ds(pl.multiple_of(t * TILE, TILE), TILE)
            term = jnp.dot(hall[block], wall[block, :, at], preferred_element_type=jnp.float32)
            if fresh:
                acc[:, at] = term
                acc[pl.ds(0, slots), at] += resv[:, at].astype(jnp.float32)
            else:
                acc[:, at] += term
            return carry

        lax.fori_loop(0, cols // TILE, tile, 0)

    loads[0].wait()
    loads[1].wait()
    add_block(me, True)

    def use(step):
        for direction in range(2):

            @pl.when(arrives(direction, step))
            def _(direction=direction):
                block = me - step if direction == 0 else me + step
                for c in range(chunks):
                    got = wpart(block, other, c)
                    remote(
                        got, got, wzs.at[0, 0, 0], wyr.at[block, c], {"groups": other}
                    ).wait_recv()
                add_block(block, False)

    for step in range(2, rows):
        for c in range(chunks):
            forward(step, c)
        use(step - 1)
    use(rows - 1)

    def finish(t, carry):
        at = pl.ds(pl.multiple_of(t * TILE, TILE), TILE)
        mixed[:, at] = acc[:, at].astype(jnp.bfloat16)
        return carry

    lax.fori_loop(0, cols // TILE, finish, 0)

    pad_images = pools.shape[1]
    image_at = lax.broadcasted_iota(jnp.int32, (pad_images, length), 0)
    member = jnp.logical_and(image_at == key_seg, image_at < images).astype(jnp.bfloat16)
    sums = jnp.dot(member, mixed[...], preferred_element_type=jnp.float32)
    image_col = lax.broadcasted_iota(jnp.int32, (pad_images, 1), 0)
    divisor = jnp.ones((pad_images, 1), jnp.float32)
    for j in range(images):
        divisor = jnp.where(image_col == j, own_counts[j].astype(jnp.float32), divisor)
    pools[me] = (sums / divisor).astype(jnp.bfloat16)

    def dp_peer(k):
        return lax.rem(me + k, rows)

    def dp_from(k):
        return lax.rem(me + rows - k, rows)

    def pcopy(k):
        return remote(pools.at[me], pools.at[me], ps.at[k], pr.at[k], {"dp": dp_peer(k)})

    for k in range(1, rows):
        pcopy(k).start()

    def mcopy(k):
        return remote(sbuf.at[k], rbuf.at[me], ms.at[k], mr.at[k], {"dp": dp_peer(k)})

    def mwait(k):
        part = rbuf.at[dp_from(k)]
        remote(part, part, ms.at[k], mr.at[k], {"dp": dp_peer(k)}).wait_recv()

    patch = lax.broadcasted_iota(jnp.int32, (pair, length), 0)
    slot = lax.broadcasted_iota(jnp.int32, (pair, length), 1)
    for k in (2, 1, 3, 0) if rows == 4 else tuple(range(1, rows)) + (0,):
        dest = dp_peer(k)
        first, count = 0, 0
        for j in range(images):
            hit = (own_plan[j] == dest).astype(jnp.int32)
            first = first + hit * starts[j]
            count = count + hit * own_counts[j]
        pick_rows = jnp.logical_and(slot == patch + first, patch < count).astype(jnp.bfloat16)

        def choose(t, carry, k=k, pick_rows=pick_rows):
            at = pl.ds(pl.multiple_of(t * TILE, TILE), TILE)
            part = jnp.dot(pick_rows, mixed[:, at], preferred_element_type=jnp.float32)
            sbuf[k, :, at] = part.astype(jnp.bfloat16)
            return carry

        lax.fori_loop(0, cols // TILE, choose, 0)
        if k:
            mcopy(k).start()

    for k in range(1, rows):
        part = pools.at[dp_from(k)]
        remote(part, part, ps.at[k], pr.at[k], {"dp": dp_peer(k)}).wait_recv()
    loads[2].wait()
    group_rows = lgs.shape[1]
    order_row = lax.broadcasted_iota(jnp.int32, (images * group_rows, rows * pad_images), 0)
    order_col = lax.broadcasted_iota(jnp.int32, (images * group_rows, rows * pad_images), 1)
    wanted = lax.rem(order_row, group_rows) * pad_images + order_row // group_rows
    order = (order_col == wanted).astype(jnp.bfloat16)
    pooled_all = pools[...].reshape(rows * pad_images, cols)
    by_image = jnp.dot(order, pooled_all, preferred_element_type=jnp.float32).astype(jnp.bfloat16)
    classes = lwv.shape[1]

    def label_tile(t, carry):
        at = pl.ds(pl.multiple_of(t * TILE, TILE), TILE)
        part = jnp.dot(by_image, lwv[:, at], preferred_element_type=jnp.float32)
        for j in range(images):
            lgs[j, :, at] = part[j * group_rows : (j + 1) * group_rows]
        return carry

    lax.fori_loop(0, classes // TILE, label_tile, 0)

    def lcopy(k):
        peer = lax.rem(mp + k, 4)
        return remote(lgs.at[peer], lrecv.at[k], ls.at[k], lr.at[k], {"mp": peer})

    for k in range(1, 4):
        lcopy(k).start()
    for k in range(1, 4):
        lcopy(k).wait_recv()
    total = lgs[mp]
    for k in range(1, 4):
        total = total + lrecv[k]
    probs = jax.nn.sigmoid(total + bias_ref[...])
    for r in range(rows):
        for t in range(classes // LANES):
            pbuf[r, pl.ds(t, 1), :] = probs[r : r + 1, t * LANES : (t + 1) * LANES]

    def bcopy(k):
        peer = dp_peer(k)
        return remote(pbuf.at[peer], precv.at[me], bs.at[k], br.at[k], {"dp": peer})

    for k in range(1, rows):
        bcopy(k).start()

    arrive, offset = [], 0
    for r in range(rows):
        count = 0
        for j in range(images):
            count = count + (plan[r, j] == me).astype(jnp.int32) * counts[r, j]
        arrive.append((offset, count))
        offset = offset + count
    for k in range(1, rows):
        mwait(k)
    rbuf[me] = sbuf[0]
    tokens = out_ref.shape[0]
    token = lax.broadcasted_iota(jnp.int32, (tokens, pair), 0)
    within = lax.broadcasted_iota(jnp.int32, (tokens, pair), 1)
    places = [
        jnp.logical_and(within == token - begin, within < count).astype(jnp.bfloat16)
        for begin, count in arrive
    ]

    def place(t, carry):
        at = pl.ds(pl.multiple_of(t * TILE, TILE), TILE)
        part = jnp.dot(places[0], rbuf[0, :, at], preferred_element_type=jnp.float32)
        for r in range(1, rows):
            part = part + jnp.dot(places[r], rbuf[r, :, at], preferred_element_type=jnp.float32)
        out_ref[:, at] = part.astype(jnp.bfloat16)
        return carry

    lax.fori_loop(0, cols // TILE, place, 0)
    for k in range(1, rows):
        part = precv.at[dp_from(k)]
        remote(part, part, bs.at[k], br.at[k], {"dp": dp_peer(k)}).wait_recv()
    precv[me] = pbuf[me]
    lab_ref[...] = precv[...]

    for p in range(pieces):
        for kind in range(3):
            hcopy(kind, p).wait_send()
    for step in range(rows):
        for direction in range(2):
            for c in range(chunks):
                if step < rows - 1:

                    @pl.when(can_send(direction, step))
                    def _(direction=direction, step=step, c=c):
                        zcopy(direction, step, c).wait_send()

                if step > 0:

                    @pl.when(arrives(direction, step))
                    def _(direction=direction, step=step, c=c):
                        ycopy(direction, step, c).wait_send()

    for k in range(1, rows):
        pcopy(k).wait_send()
        mcopy(k).wait_send()
        bcopy(k).wait_send()
    for k in range(1, 4):
        lcopy(k).wait_send()


def round_up(value, step):
    return -(-value // step) * step


def fused(
    qkv_home,
    resid_home,
    out_weight,
    label_weight,
    label_bias,
    query_gain,
    key_gain,
    patch_counts,
    move_plan,
):
    rows = lax.axis_size("dp")
    slots, width = qkv_home.shape[1], qkv_home.shape[3]
    depth, cols = out_weight.shape
    classes = label_weight.shape[1]
    length = round_up(slots, TILE)
    pair = round_up(slots // rows, 16)
    padded = jnp.pad(qkv_home[0], ((0, length - slots), (0, 0), (0, 0)))
    queries, keys, values = padded[:, 0], padded[:, 1], padded[:, 2]
    chunks, pieces = depth // TILE, width // TILE
    bf16, f32 = jnp.bfloat16, jnp.float32
    vmem = pl.BlockSpec(memory_space=pltpu.VMEM)
    smem = pl.BlockSpec(memory_space=pltpu.SMEM)
    hbm = pl.BlockSpec(memory_space=pl.ANY)
    dma = pltpu.SemaphoreType.DMA
    mixed, labels = pl.pallas_call(
        functools.partial(block_kernel, (rows, slots, pair)),
        out_shape=(
            jax.ShapeDtypeStruct((TOK, cols), bf16),
            jax.ShapeDtypeStruct((rows, classes // LANES, LANES), f32),
        ),
        in_specs=[smem, smem, vmem, vmem, vmem, vmem, vmem, vmem, hbm, hbm, hbm],
        out_specs=(vmem, vmem),
        scratch_shapes=[
            pltpu.VMEM((length, width), bf16),
            pltpu.VMEM((length, width), bf16),
            pltpu.VMEM((4, length, width), bf16),
            pltpu.VMEM((rows, depth, cols), bf16),
            pltpu.VMEM((length, cols), f32),
            pltpu.VMEM((length, cols), bf16),
            pltpu.VMEM((rows, pair, cols), bf16),
            pltpu.VMEM((rows, pair, cols), bf16),
            pltpu.VMEM(label_weight.shape, bf16),
            pltpu.VMEM((slots, cols), bf16),
            pltpu.VMEM((rows, 16, cols), bf16),
            pltpu.VMEM((rows, 8, classes), f32),
            pltpu.VMEM((4, 8, classes), f32),
            pltpu.VMEM((rows, classes // LANES, LANES), f32),
            pltpu.VMEM((rows, classes // LANES, LANES), f32),
            dma((3,)),
            dma((3, pieces)),
            dma((3, pieces)),
            dma((2, rows, chunks)),
            dma((rows, chunks)),
            dma((2, rows, chunks)),
            dma((rows, chunks)),
            dma((rows,)),
            dma((rows,)),
            dma((rows,)),
            dma((rows,)),
            dma((4,)),
            dma((4,)),
            dma((rows,)),
            dma((rows,)),
        ],
        compiler_params=pltpu.CompilerParams(
            collective_id=0, has_side_effects=True, vmem_limit_bytes=63 * 1024 * 1024
        ),
    )(
        patch_counts,
        move_plan,
        queries,
        keys,
        values,
        label_bias[None],
        query_gain[None],
        key_gain[None],
        resid_home[0],
        out_weight,
        label_weight,
    )
    return (mixed[None], labels.reshape(1, 1, rows * classes))


def on_device(
    qkv_home,
    resid_home,
    out_weight,
    label_weight,
    label_bias,
    query_gain,
    key_gain,
    patch_counts,
    move_plan,
    segment_ids,
):
    row_count = lax.axis_size("dp")
    if row_count == lax.axis_size("mp") == 4 and lax.axis_size("groups") == 2:
        return fused(
            qkv_home,
            resid_home,
            out_weight,
            label_weight,
            label_bias,
            query_gain,
            key_gain,
            patch_counts,
            move_plan,
        )
    my_index = lax.axis_index("dp")
    home_slots = segment_ids.shape[1]
    pair_slots = home_slots // row_count
    image_ids = lax.broadcasted_iota(jnp.int32, (row_count, row_count, row_count), 2)
    image_ends = jnp.cumsum(patch_counts, axis=1)
    starts = image_ends - patch_counts
    matches = (move_plan[:, :, None] == image_ids).astype(jnp.int32)
    image_sizes = jnp.sum(patch_counts[:, :, None] * matches, axis=1)
    firsts = jnp.sum(starts[:, :, None] * matches, axis=1)
    send_sizes = lax.dynamic_index_in_dim(image_sizes, my_index, 0, keepdims=False)
    send_firsts = lax.dynamic_index_in_dim(firsts, my_index, 0, keepdims=False)
    within = lax.broadcasted_iota(jnp.int32, (row_count, pair_slots), 1)
    send_valid = within < send_sizes[:, None]
    send_index = jnp.minimum(send_firsts[:, None] + within, home_slots - 1).reshape(-1)
    arrive_sizes = lax.dynamic_index_in_dim(image_sizes, my_index, 1, keepdims=False)
    arrive_ends = jnp.cumsum(arrive_sizes)
    arrive_starts = arrive_ends - arrive_sizes
    slot_grid = lax.broadcasted_iota(jnp.int32, (TOK, row_count), 0)
    source = jnp.sum((slot_grid >= arrive_ends[None, :]).astype(jnp.int32), axis=1)
    chosen = (source[:, None] == lax.broadcasted_iota(jnp.int32, (TOK, row_count), 1)).astype(
        jnp.int32
    )
    arrive_index = (
        source * pair_slots + slot_grid[:, 0] - jnp.sum(chosen * arrive_starts[None, :], axis=1)
    )
    home_mixed = project(
        attend(qkv_home[0], segment_ids[0], query_gain, key_gain), resid_home[0], out_weight
    )
    count_row = lax.dynamic_index_in_dim(patch_counts, my_index, 0, keepdims=False)
    pooled = pool(home_mixed, segment_ids[0], count_row)
    partial_value = label_terms(pooled, label_weight)
    send_mixed = pick(home_mixed, send_index, send_valid)
    got_mixed = lax.all_to_all(send_mixed, "dp", split_axis=0, concat_axis=0, tiled=True)
    mixed = jnp.take(got_mixed.reshape(row_count * pair_slots, -1), arrive_index, axis=0)
    logit_sums = lax.psum_scatter(
        partial_value.astype(jnp.bfloat16), "mp", scatter_dimension=1, tiled=True
    ).astype(jnp.float32)
    class_probs = jax.nn.sigmoid(logit_sums + label_bias[None, None, :])
    labels = lax.all_to_all(
        class_probs.astype(jnp.bfloat16), "dp", split_axis=0, concat_axis=2, tiled=True
    ).astype(class_probs.dtype)
    return (mixed[None], labels)


def solution(mesh):
    return jax.shard_map(
        on_device,
        mesh=mesh,
        in_specs=(
            P(("groups", "dp"), None, None, "mp"),
            P(("groups", "dp"), None, "mp"),
            P("dp", "mp"),
            P("mp", "dp"),
            P("dp"),
            P(),
            P(),
            P("groups", None),
            P("groups", None),
            P(("groups", "dp"), None),
        ),
        out_specs=(P(("groups", "dp"), None, "mp"), P(("groups", "dp"), "mp", None)),
        check_vma=False,
    )
```

```python
import functools
import math

import jax
import jax.numpy as jnp
from jax import lax
from jax.experimental import pallas as pl
from jax.experimental.pallas import tpu as pltpu
from jax.sharding import PartitionSpec as P

TOK = 384


EPSILON = 1e-06


def head_norm(values, norm_gain):
    center = values - jnp.mean(values, axis=-1, keepdims=True)
    spread = jnp.mean(center * center, axis=-1, keepdims=True)
    return center * lax.rsqrt(spread + EPSILON) * norm_gain


def attend(qkv_rows, seg_rows, query_gain, key_gain):
    length = qkv_rows.shape[0]
    head_width = query_gain.shape[0]
    head_count = qkv_rows.shape[2] // head_width
    split_parts = qkv_rows.reshape(length, 3, head_count, head_width)
    queries = head_norm(split_parts[:, 0].astype(jnp.float32), query_gain).astype(jnp.bfloat16)
    key_rows = head_norm(split_parts[:, 1].astype(jnp.float32), key_gain).astype(jnp.bfloat16)
    scores = jnp.einsum(
        "qhd,khd->hqk", queries, key_rows, preferred_element_type=jnp.float32
    ) / math.sqrt(head_width)
    same_image = seg_rows[:, None] == seg_rows[None, :]
    raised = jnp.where(same_image[None], jnp.exp(scores), 0.0)
    weights = (raised / jnp.sum(raised, axis=-1, keepdims=True)).astype(jnp.bfloat16)
    head_out = jnp.einsum(
        "hqk,khd->qhd", weights, split_parts[:, 2], preferred_element_type=jnp.float32
    )
    return head_out.reshape(length, head_count * head_width).astype(jnp.bfloat16)


def project(heads_local, resid_rows, out_weight):
    gathered = lax.all_gather(heads_local, "mp", axis=1, tiled=True)
    running = resid_rows.astype(jnp.float32) + jnp.dot(
        gathered,
        lax.all_gather(out_weight, "dp", axis=0, tiled=True),
        preferred_element_type=jnp.float32,
    )
    return running.astype(jnp.bfloat16)


def pool(row_mixed, seg_rows, count_row):
    images = count_row.shape[0]
    member_ids = lax.broadcasted_iota(jnp.int32, (images, seg_rows.shape[0]), 0)
    member = (member_ids == seg_rows[None, :]).astype(jnp.bfloat16)
    image_sums = jnp.dot(member, row_mixed, preferred_element_type=jnp.float32)
    return (image_sums / count_row[:, None].astype(jnp.float32)).astype(jnp.bfloat16)


def label_terms(pooled, label_weight):
    return jnp.einsum(
        "abd,dc->abc",
        lax.all_gather(pooled[None], "dp", axis=0, tiled=True),
        label_weight,
        preferred_element_type=jnp.float32,
    )


def pick(values, row_index, is_valid):
    taken = jnp.take(values, row_index, axis=0)
    taken = taken.reshape(is_valid.shape + values.shape[1:])
    keep_mask = is_valid.reshape(is_valid.shape + (1,) * (values.ndim - 1))
    return jnp.where(keep_mask, taken, jnp.zeros_like(taken))


MESH = pl.DeviceIdType.MESH
LANES = 128
TILE = 256


def remote(src, dst, send_sem, recv_sem, where):
    return pltpu.make_async_remote_copy(
        src_ref=src,
        dst_ref=dst,
        send_sem=send_sem,
        recv_sem=recv_sem,
        device_id=where,
        device_id_type=MESH,
    )


def normed(values, gain):
    values = values.astype(jnp.float32)
    center = values - jnp.mean(values, axis=-1, keepdims=True)
    spread = jnp.mean(center * center, axis=-1, keepdims=True)
    return (center * lax.rsqrt(spread + EPSILON) * gain).astype(jnp.bfloat16)


def block_kernel(
    sizes,
    counts,
    plan,
    bias_ref,
    qg_ref,
    kg_ref,
    qkv_hbm,
    resid_hbm,
    w_hbm,
    lw_hbm,
    out_ref,
    lab_ref,
    raw,
    nq,
    nk,
    nv,
    hall,
    wall,
    acc,
    mixed,
    sbuf,
    rbuf,
    lwv,
    resv,
    pools,
    lgs,
    lrecv,
    pbuf,
    precv,
    load_sem,
    hs,
    hr,
    wzs,
    wzr,
    wys,
    wyr,
    ps,
    pr,
    ms,
    mr,
    ls,
    lr,
    bs,
    br,
):
    rows, slots, pair, length, phases = sizes
    me = lax.axis_index("dp")
    mp = lax.axis_index("mp")
    group = lax.axis_index("groups")
    other = 1 - group
    core = lax.rem(mp, 2)
    near = mp + 1 - 2 * core
    side = lax.rem(mp + 2, 4)
    far = lax.rem(near + 2, 4)
    width = raw.shape[2]
    depth, cols = w_hbm.shape
    span = cols // phases
    half = span // 2
    pieces = width // TILE
    images = rows

    loads = [
        pltpu.make_async_copy(qkv_hbm, raw, load_sem.at[3]),
        pltpu.make_async_copy(w_hbm, wall.at[me], load_sem.at[0]),
        pltpu.make_async_copy(resid_hbm, resv, load_sem.at[1]),
        pltpu.make_async_copy(lw_hbm, lwv, load_sem.at[2]),
    ]
    for load in loads:
        load.start()

    barrier = pltpu.get_barrier_semaphore()
    for k in range(1, 4):
        pl.semaphore_signal(
            barrier, inc=1, device_id={"mp": lax.rem(mp + k, 4)}, device_id_type=MESH
        )
    for k in range(1, rows):
        pl.semaphore_signal(
            barrier, inc=1, device_id={"dp": lax.rem(me + k, rows)}, device_id_type=MESH
        )
    pl.semaphore_signal(barrier, inc=1, device_id={"groups": other}, device_id_type=MESH)
    pl.semaphore_wait(barrier, 3 + rows - 1 + 1)

    def share(phase, which):
        return pl.ds(pl.multiple_of(phase * span + which * half, half), half)

    def wpart(block, phase, which, c):
        return wall.at[block, pl.ds(c * TILE, TILE), share(phase, which)]

    def source(direction, step):
        return me - step if direction == 0 else me + step

    def zcopy(direction, phase, step, c):
        block = source(direction, step)
        part = wpart(block, phase, group, c)
        own = w_hbm.at[pl.ds(c * TILE, TILE), share(phase, group)]
        return remote(
            own if step == 0 else part,
            part,
            wzs.at[direction, phase, step, c],
            wzr.at[phase, block, c],
            {"dp": me + 1 if direction == 0 else me - 1},
        )

    def can_send(direction, step):
        if direction == 0:
            return jnp.logical_and(me - step >= 0, me < rows - 1)
        return jnp.logical_and(me + step < rows, me > 0)

    def arrives(direction, step):
        return me - step >= 0 if direction == 0 else me + step < rows

    def ycopy(direction, phase, step, c):
        block = source(direction, step)
        part = wpart(block, phase, group, c)
        return remote(
            part,
            part,
            wys.at[direction, phase, step, c],
            wyr.at[phase, block, c],
            {"groups": other},
        )

    chunks = depth // TILE

    def send_own(phase):
        for c in range(chunks):
            for direction in range(2):

                @pl.when(can_send(direction, 0))
                def _(direction=direction, c=c):
                    zcopy(direction, phase, 0, c).start()

    def forward(phase, step, c):
        for direction in range(2):

            @pl.when(arrives(direction, step))
            def _(direction=direction):
                block = source(direction, step)
                got = wpart(block, phase, group, c)
                remote(
                    got, got, wzs.at[0, 0, 0, 0], wzr.at[phase, block, c], {"groups": other}
                ).wait_recv()
                if step < rows - 1:

                    @pl.when(can_send(direction, step))
                    def _():
                        zcopy(direction, phase, step, c).start()

                ycopy(direction, phase, step, c).start()

    send_own(0)

    own_counts = [counts[me, j] for j in range(images)]
    own_plan = [plan[me, j] for j in range(images)]
    ends, starts, running = [], [], 0
    for j in range(images):
        starts.append(running)
        running = running + own_counts[j]
        ends.append(running)

    def segment(index):
        total = jnp.zeros(index.shape, jnp.int32)
        for j in range(images):
            total = total + (index >= ends[j]).astype(jnp.int32)
        return total

    key_seg = segment(lax.broadcasted_iota(jnp.int32, (1, length), 1))
    heads = width // LANES
    q_gain = qg_ref[...]
    k_gain = kg_ref[...]

    def norm_head(h, carry):
        at = pl.ds(pl.multiple_of(h * LANES, LANES), LANES)
        nq[pl.ds(0, slots), at] = normed(raw[0, :, at], q_gain)
        nk[pl.ds(0, slots), at] = normed(raw[1, :, at], k_gain)
        nv[pl.ds(0, slots), at] = raw[2, :, at]
        return carry

    if length > slots:
        low = slots // 16 * 16
        for ref in (nq, nk, nv):
            ref[pl.ds(low, length - low), :] = jnp.zeros((length - low, width), jnp.bfloat16)
    loads[0].wait()
    lax.fori_loop(0, heads, norm_head, 0)
    scale = math.log2(math.e) / math.sqrt(LANES)
    per_head = length // TILE

    def hcopy(kind, p):
        at = pl.ds(p * TILE, TILE)
        block = side if kind == 2 else mp
        part = hall.at[block, :, at]
        peer = side if kind == 1 else near
        return remote(part, part, hs.at[kind, p], hr.at[kind, p], {"mp": peer})

    def hwait(kind, p):
        block = (near, side, far)[kind]
        part = hall.at[block, :, pl.ds(p * TILE, TILE)]
        remote(part, part, hs.at[kind, p], hr.at[kind, p], {"mp": near}).wait_recv()

    for p in range(pieces):

        def attend_part(i, carry, p=p):
            h = p * (TILE // LANES) + i // per_head
            first = pl.multiple_of(lax.rem(i, per_head) * TILE, TILE)
            at = pl.ds(pl.multiple_of(h * LANES, LANES), LANES)
            scores = lax.dot_general(
                nq[pl.ds(first, TILE), at],
                nk[:, at],
                (((1,), (1,)), ((), ())),
                preferred_element_type=jnp.float32,
            )
            query_seg = segment(lax.broadcasted_iota(jnp.int32, (TILE, 1), 0) + first)
            raised = jnp.where(query_seg == key_seg, jnp.exp2(scores * scale), 0.0)
            total = jnp.sum(raised, axis=-1, keepdims=True)
            weights = (raised * (1.0 / total)).astype(jnp.bfloat16)
            result = jnp.dot(weights, nv[:, at], preferred_element_type=jnp.float32)
            hall[mp, pl.ds(first, TILE), at] = result.astype(jnp.bfloat16)
            return carry

        lax.fori_loop(0, (TILE // LANES) * per_head, attend_part, 0)
        hcopy(1, p).start()
        hcopy(0, p).start()
        if p < chunks:
            forward(0, 1, p)
    for c in range(pieces, chunks):
        forward(0, 1, c)
    if phases > 1:
        send_own(1)
    for p in range(pieces):
        hwait(1, p)
        hcopy(2, p).start()

    def add_block(block, phase, fresh):
        def tile(t, carry):
            at = pl.ds(pl.multiple_of(phase * span + t * TILE, TILE), TILE)
            term = jnp.dot(hall[block], wall[block, :, at], preferred_element_type=jnp.float32)
            if fresh:
                acc[:, at] = term
                acc[pl.ds(0, slots), at] += resv[:, at].astype(jnp.float32)
            else:
                acc[:, at] += term
            return carry

        lax.fori_loop(0, span // TILE, tile, 0)

    def use(phase, step):
        if step == 0:
            add_block(me, phase, True)
            return
        for direction in range(2):

            @pl.when(arrives(direction, step))
            def _(direction=direction):
                block = source(direction, step)
                for c in range(chunks):
                    got = wpart(block, phase, other, c)
                    remote(
                        got, got, wzs.at[0, 0, 0, 0], wyr.at[phase, block, c], {"groups": other}
                    ).wait_recv()
                add_block(block, phase, False)

    pad_images = pools.shape[1]
    image_at = lax.broadcasted_iota(jnp.int32, (pad_images, length), 0)
    member = jnp.logical_and(image_at == key_seg, image_at < images).astype(jnp.bfloat16)
    image_col = lax.broadcasted_iota(jnp.int32, (pad_images, 1), 0)
    divisor = jnp.ones((pad_images, 1), jnp.float32)
    for j in range(images):
        divisor = jnp.where(image_col == j, own_counts[j].astype(jnp.float32), divisor)

    def dp_peer(k):
        return lax.rem(me + k, rows)

    def dp_from(k):
        return lax.rem(me + rows - k, rows)

    def pcopy(k):
        return remote(pools.at[me], pools.at[me], ps.at[k], pr.at[k], {"dp": dp_peer(k)})

    def columns(phase):
        return pl.ds(phase * span, span)

    def mcopy(phase, k):
        at = columns(phase)
        return remote(
            sbuf.at[k, :, at],
            rbuf.at[me, :, at],
            ms.at[phase, k],
            mr.at[phase, k],
            {"dp": dp_peer(k)},
        )

    def mwait(phase, k):
        part = rbuf.at[dp_from(k), :, columns(phase)]
        remote(part, part, ms.at[phase, k], mr.at[phase, k], {"dp": dp_peer(k)}).wait_recv()

    patch = lax.broadcasted_iota(jnp.int32, (pair, length), 0)
    slot = lax.broadcasted_iota(jnp.int32, (pair, length), 1)
    far_first = sorted(range(1, rows), key=lambda k: -min(k, rows - k))

    def finish(phase):
        def pool_tile(t, carry):
            at = pl.ds(pl.multiple_of(phase * span + t * TILE, TILE), TILE)
            values = acc[:, at].astype(jnp.bfloat16)
            mixed[:, at] = values
            sums = jnp.dot(member, values, preferred_element_type=jnp.float32)
            pools[me, :, at] = (sums / divisor).astype(jnp.bfloat16)
            return carry

        lax.fori_loop(0, span // TILE, pool_tile, 0)
        if phase == phases - 1:
            for k in range(1, rows):
                pcopy(k).start()
        for k in far_first + [0]:
            dest = dp_peer(k)
            first, count = 0, 0
            for j in range(images):
                hit = (own_plan[j] == dest).astype(jnp.int32)
                first = first + hit * starts[j]
                count = count + hit * own_counts[j]
            pick_rows = jnp.logical_and(slot == patch + first, patch < count).astype(jnp.bfloat16)

            def choose(t, carry, k=k, pick_rows=pick_rows):
                at = pl.ds(pl.multiple_of(phase * span + t * TILE, TILE), TILE)
                part = jnp.dot(pick_rows, mixed[:, at], preferred_element_type=jnp.float32)
                if k:
                    sbuf[k, :, at] = part.astype(jnp.bfloat16)
                else:
                    rbuf[me, :, at] = part.astype(jnp.bfloat16)
                return carry

            lax.fori_loop(0, span // TILE, choose, 0)
            if k:
                mcopy(phase, k).start()

    events = [(phase, step) for phase in range(phases) for step in range(1, rows)]
    events.sort(key=lambda e: (2 * e[0] + e[1], -e[0]))
    ready = False
    waiting = [(0, 1)]
    done = set()

    def consume(phase, step):
        nonlocal ready
        if not ready:
            for p in range(pieces):
                hwait(0, p)
                hwait(2, p)
            loads[1].wait()
            loads[2].wait()
            ready = True
        if (phase, 0) not in done:
            done.add((phase, 0))
            use(phase, 0)
        use(phase, step)
        done.add((phase, step))
        if all((phase, i) in done for i in range(rows)):
            finish(phase)

    for phase, step in events[1:]:
        if step == 2 and phase > 0 and phase + 1 < phases:
            send_own(phase + 1)
        for c in range(chunks):
            forward(phase, step, c)
        waiting.append((phase, step))
        if len(waiting) > 2:
            consume(*waiting.pop(0))
    for phase, step in waiting:
        consume(phase, step)

    for k in range(1, rows):
        part = pools.at[dp_from(k)]
        remote(part, part, ps.at[k], pr.at[k], {"dp": dp_peer(k)}).wait_recv()
    loads[3].wait()
    group_rows = lgs.shape[1]
    order_row = lax.broadcasted_iota(jnp.int32, (images * group_rows, rows * pad_images), 0)
    order_col = lax.broadcasted_iota(jnp.int32, (images * group_rows, rows * pad_images), 1)
    wanted = lax.rem(order_row, group_rows) * pad_images + order_row // group_rows
    order = (order_col == wanted).astype(jnp.bfloat16)
    pooled_all = pools[...].reshape(rows * pad_images, cols)
    by_image = jnp.dot(order, pooled_all, preferred_element_type=jnp.float32).astype(jnp.bfloat16)
    classes = lwv.shape[1]

    def label_tile(t, carry):
        at = pl.ds(pl.multiple_of(t * TILE, TILE), TILE)
        part = jnp.dot(by_image, lwv[:, at], preferred_element_type=jnp.float32)
        for j in range(images):
            lgs[j, :, at] = part[j * group_rows : (j + 1) * group_rows]
        return carry

    lax.fori_loop(0, classes // TILE, label_tile, 0)

    def lcopy(k):
        peer = lax.rem(mp + k, 4)
        return remote(lgs.at[peer], lrecv.at[k], ls.at[k], lr.at[k], {"mp": peer})

    for k in range(1, 4):
        lcopy(k).start()
    for k in range(1, 4):
        lcopy(k).wait_recv()
    total = lgs[mp]
    for k in range(1, 4):
        total = total + lrecv[k]
    probs = jax.nn.sigmoid(total + bias_ref[...])
    for r in range(rows):
        for t in range(classes // LANES):
            pbuf[r, pl.ds(t, 1), :] = probs[r : r + 1, t * LANES : (t + 1) * LANES]

    def bcopy(k):
        peer = dp_peer(k)
        return remote(pbuf.at[peer], precv.at[me], bs.at[k], br.at[k], {"dp": peer})

    for k in range(1, rows):
        bcopy(k).start()

    arrive, offset = [], 0
    for r in range(rows):
        count = 0
        for j in range(images):
            count = count + (plan[r, j] == me).astype(jnp.int32) * counts[r, j]
        arrive.append((offset, count))
        offset = offset + count
    tokens = out_ref.shape[0]
    token = lax.broadcasted_iota(jnp.int32, (tokens, pair), 0)
    within = lax.broadcasted_iota(jnp.int32, (tokens, pair), 1)
    places = [
        jnp.logical_and(within == token - begin, within < count).astype(jnp.bfloat16)
        for begin, count in arrive
    ]

    def place(t, carry, phase=0):
        at = pl.ds(pl.multiple_of(phase * span + t * TILE, TILE), TILE)
        part = jnp.dot(places[0], rbuf[0, :, at], preferred_element_type=jnp.float32)
        for r in range(1, rows):
            part = part + jnp.dot(places[r], rbuf[r, :, at], preferred_element_type=jnp.float32)
        out_ref[:, at] = part.astype(jnp.bfloat16)
        return carry

    for phase in range(phases):
        for k in range(1, rows):
            mwait(phase, k)
        lax.fori_loop(0, span // TILE, functools.partial(place, phase=phase), 0)
    for k in range(1, rows):
        part = precv.at[dp_from(k)]
        remote(part, part, bs.at[k], br.at[k], {"dp": dp_peer(k)}).wait_recv()
    precv[me] = pbuf[me]
    lab_ref[...] = precv[...]

    for p in range(pieces):
        for kind in range(3):
            hcopy(kind, p).wait_send()
    for phase in range(phases):
        for k in range(1, rows):
            mcopy(phase, k).wait_send()
        for step in range(rows):
            for direction in range(2):
                for c in range(chunks):
                    if step < rows - 1:

                        @pl.when(can_send(direction, step))
                        def _(phase=phase, direction=direction, step=step, c=c):
                            zcopy(direction, phase, step, c).wait_send()

                    if step > 0:

                        @pl.when(arrives(direction, step))
                        def _(phase=phase, direction=direction, step=step, c=c):
                            ycopy(direction, phase, step, c).wait_send()

    for k in range(1, rows):
        pcopy(k).wait_send()
        bcopy(k).wait_send()
    for k in range(1, 4):
        lcopy(k).wait_send()


def round_up(value, step):
    return -(-value // step) * step


def fused(
    qkv_home,
    resid_home,
    out_weight,
    label_weight,
    label_bias,
    query_gain,
    key_gain,
    patch_counts,
    move_plan,
):
    rows = lax.axis_size("dp")
    slots, width = qkv_home.shape[1], qkv_home.shape[3]
    depth, cols = out_weight.shape
    classes = label_weight.shape[1]
    length = round_up(slots, TILE)
    pair = round_up(slots // rows, 16)
    phases = 2
    chunks, pieces = depth // TILE, width // TILE
    bf16, f32 = jnp.bfloat16, jnp.float32
    vmem = pl.BlockSpec(memory_space=pltpu.VMEM)
    smem = pl.BlockSpec(memory_space=pltpu.SMEM)
    hbm = pl.BlockSpec(memory_space=pl.ANY)
    dma = pltpu.SemaphoreType.DMA
    mixed, labels = pl.pallas_call(
        functools.partial(block_kernel, (rows, slots, pair, length, phases)),
        out_shape=(
            jax.ShapeDtypeStruct((TOK, cols), bf16),
            jax.ShapeDtypeStruct((rows, classes // LANES, LANES), f32),
        ),
        in_specs=[smem, smem, vmem, vmem, vmem, hbm, hbm, hbm, hbm],
        out_specs=(vmem, vmem),
        scratch_shapes=[
            pltpu.VMEM((3, slots, width), bf16),
            pltpu.VMEM((length, width), bf16),
            pltpu.VMEM((length, width), bf16),
            pltpu.VMEM((length, width), bf16),
            pltpu.VMEM((4, length, width), bf16),
            pltpu.VMEM((rows, depth, cols), bf16),
            pltpu.VMEM((length, cols), f32),
            pltpu.VMEM((length, cols), bf16),
            pltpu.VMEM((rows, pair, cols), bf16),
            pltpu.VMEM((rows, pair, cols), bf16),
            pltpu.VMEM(label_weight.shape, bf16),
            pltpu.VMEM((slots, cols), bf16),
            pltpu.VMEM((rows, 16, cols), bf16),
            pltpu.VMEM((rows, 8, classes), f32),
            pltpu.VMEM((4, 8, classes), f32),
            pltpu.VMEM((rows, classes // LANES, LANES), f32),
            pltpu.VMEM((rows, classes // LANES, LANES), f32),
            dma((4,)),
            dma((3, pieces)),
            dma((3, pieces)),
            dma((2, phases, rows, chunks)),
            dma((phases, rows, chunks)),
            dma((2, phases, rows, chunks)),
            dma((phases, rows, chunks)),
            dma((rows,)),
            dma((rows,)),
            dma((phases, rows)),
            dma((phases, rows)),
            dma((4,)),
            dma((4,)),
            dma((rows,)),
            dma((rows,)),
        ],
        compiler_params=pltpu.CompilerParams(
            collective_id=0, has_side_effects=True, vmem_limit_bytes=63 * 1024 * 1024
        ),
    )(
        patch_counts,
        move_plan,
        label_bias[None],
        query_gain[None],
        key_gain[None],
        jnp.transpose(qkv_home[0], (1, 0, 2)),
        resid_home[0],
        out_weight,
        label_weight,
    )
    return (mixed[None], labels.reshape(1, 1, rows * classes))


def on_device(
    qkv_home,
    resid_home,
    out_weight,
    label_weight,
    label_bias,
    query_gain,
    key_gain,
    patch_counts,
    move_plan,
    segment_ids,
):
    row_count = lax.axis_size("dp")
    if row_count == lax.axis_size("mp") == 4 and lax.axis_size("groups") == 2:
        return fused(
            qkv_home,
            resid_home,
            out_weight,
            label_weight,
            label_bias,
            query_gain,
            key_gain,
            patch_counts,
            move_plan,
        )
    my_index = lax.axis_index("dp")
    home_slots = segment_ids.shape[1]
    pair_slots = home_slots // row_count
    image_ids = lax.broadcasted_iota(jnp.int32, (row_count, row_count, row_count), 2)
    image_ends = jnp.cumsum(patch_counts, axis=1)
    starts = image_ends - patch_counts
    matches = (move_plan[:, :, None] == image_ids).astype(jnp.int32)
    image_sizes = jnp.sum(patch_counts[:, :, None] * matches, axis=1)
    firsts = jnp.sum(starts[:, :, None] * matches, axis=1)
    send_sizes = lax.dynamic_index_in_dim(image_sizes, my_index, 0, keepdims=False)
    send_firsts = lax.dynamic_index_in_dim(firsts, my_index, 0, keepdims=False)
    within = lax.broadcasted_iota(jnp.int32, (row_count, pair_slots), 1)
    send_valid = within < send_sizes[:, None]
    send_index = jnp.minimum(send_firsts[:, None] + within, home_slots - 1).reshape(-1)
    arrive_sizes = lax.dynamic_index_in_dim(image_sizes, my_index, 1, keepdims=False)
    arrive_ends = jnp.cumsum(arrive_sizes)
    arrive_starts = arrive_ends - arrive_sizes
    slot_grid = lax.broadcasted_iota(jnp.int32, (TOK, row_count), 0)
    source = jnp.sum((slot_grid >= arrive_ends[None, :]).astype(jnp.int32), axis=1)
    chosen = (source[:, None] == lax.broadcasted_iota(jnp.int32, (TOK, row_count), 1)).astype(
        jnp.int32
    )
    arrive_index = (
        source * pair_slots + slot_grid[:, 0] - jnp.sum(chosen * arrive_starts[None, :], axis=1)
    )
    home_mixed = project(
        attend(qkv_home[0], segment_ids[0], query_gain, key_gain), resid_home[0], out_weight
    )
    count_row = lax.dynamic_index_in_dim(patch_counts, my_index, 0, keepdims=False)
    pooled = pool(home_mixed, segment_ids[0], count_row)
    partial_value = label_terms(pooled, label_weight)
    send_mixed = pick(home_mixed, send_index, send_valid)
    got_mixed = lax.all_to_all(send_mixed, "dp", split_axis=0, concat_axis=0, tiled=True)
    mixed = jnp.take(got_mixed.reshape(row_count * pair_slots, -1), arrive_index, axis=0)
    logit_sums = lax.psum_scatter(
        partial_value.astype(jnp.bfloat16), "mp", scatter_dimension=1, tiled=True
    ).astype(jnp.float32)
    class_probs = jax.nn.sigmoid(logit_sums + label_bias[None, None, :])
    labels = lax.all_to_all(
        class_probs.astype(jnp.bfloat16), "dp", split_axis=0, concat_axis=2, tiled=True
    ).astype(class_probs.dtype)
    return (mixed[None], labels)


def solution(mesh):
    return jax.shard_map(
        on_device,
        mesh=mesh,
        in_specs=(
            P(("groups", "dp"), None, None, "mp"),
            P(("groups", "dp"), None, "mp"),
            P("dp", "mp"),
            P("mp", "dp"),
            P("dp"),
            P(),
            P(),
            P("groups", None),
            P("groups", None),
            P(("groups", "dp"), None),
        ),
        out_specs=(P(("groups", "dp"), None, "mp"), P(("groups", "dp"), "mp", None)),
        check_vma=False,
    )
```
